32 devices in a mesh: dp: 16 (over z, x, core), tensor: 2 (over y).
Axes of the slice: x: 2, y: 2, z: 4, core: 2. Of those that a mesh axis runs over, the one named last changes fastest.
Arguments:
- tokens: float32 [11008, 1024], P('dp'), may hold values from -6 to 6
- cotangent: float32 [11008, 1024], P('dp'), may hold values from -6 to 6
- ln1_gain: float32 [1024], P('dp'), may hold values from 0.5 to 1.5
- qkv_weight: float32 [1024, 3, 1024], P('dp', None, 'tensor')
- attn_out_weight: float32 [1024, 1024], P('tensor', 'dp'), may hold values from -3 to 3
- ln2_gain: float32 [1024], P('dp'), may hold values from 0.5 to 1.5
- ff_in_weight: float32 [1024, 2, 2624], P('dp', None, 'tensor'), may hold values from -0.1875 to 0.1875
- ff_out_weight: float32 [2624, 1024], P('tensor', 'dp'), may hold values from -0.125 to 0.125
- segment_ids: int32 [16, 688], P('dp'), may hold values from 0 to 2, as said below
- positions: int32 [16, 688], P('dp'), may hold values from 0 to 687, as said below
Outputs:
- output: float32 [11008, 1024], P('dp')
- input_grad: float32 [11008, 1024], P('dp')
- ln1_gain_grad: float32 [1024], P('dp')
- qkv_weight_grad: float32 [1024, 3, 1024], P('dp', None, 'tensor')
- attn_out_grad: float32 [1024, 1024], P('tensor', 'dp')
- ln2_gain_grad: float32 [1024], P('dp')
- ff_in_grad: float32 [1024, 2, 2624], P('dp', None, 'tensor')
- ff_out_grad: float32 [2624, 1024], P('tensor', 'dp')
The draws below stay inside these ranges and needn't reach their ends.
Inputs may be any that keep to these rules, and one draw needn't show every extreme that they name: `segment_ids`: each sequence packs one to three documents of 200 to 688 tokens; segment numbers count its documents from 0 in order. `positions`: each token's offset from the first token of its document.
All inputs are finite; a program needn't handle non-finite values.
Results may differ from the reference program's by a relative error of at most 0.0003.
Values sent between devices are 32-bit elements; how exact they have to be, the bound alone decides.
No kernel may reach another device: no remote copies, remote signals or barrier semaphores. Data moves between devices by JAX's collectives and lax.ppermute only.
A program may use at most 256 MiB of HBM per device.

```python
import jax
import jax.numpy as jnp
from jax import lax

D = 1024
H = 16
HD = 64
FF = 2624
SEQ = 688
DOC_MIN = 200
SEQS = 16
TOKENS = 11008


def doc_layout(base_key):
    layout_key = jax.random.fold_in(base_key, 4242)
    count_key, first_key, second_key = jax.random.split(layout_key, 3)
    doc_count = jax.random.randint(count_key, (SEQS,), 1, 4).astype(jnp.int32)
    doc_count = doc_count.at[0].set(1).at[1].set(3)
    spare = SEQ - doc_count * DOC_MIN
    first_bits = jax.random.randint(first_key, (SEQS,), 0, 1 << 30).astype(jnp.int32)
    second_bits = jax.random.randint(second_key, (SEQS,), 0, 1 << 30).astype(jnp.int32)
    first_extra = first_bits % (spare + 1)
    first_extra = first_extra.at[1].set(0)
    second_extra = second_bits % (spare - first_extra + 1)
    first_end = jnp.where(doc_count == 1, SEQ, DOC_MIN + first_extra)
    second_end = jnp.where(doc_count == 3, first_end + DOC_MIN + second_extra, SEQ)
    spots = jnp.arange(SEQ, dtype=jnp.int32)[None, :]
    seg_table = (spots >= first_end[:, None]).astype(jnp.int32) + (spots >= second_end[:, None]).astype(jnp.int32)
    starts = jnp.where(seg_table == 0, 0, jnp.where(seg_table == 1, first_end[:, None], second_end[:, None]))
    return (seg_table, (spots - starts).astype(jnp.int32))


def draw_segment_ids(key, part):
    return doc_layout(key)[0]


def draw_positions(key, part):
    return doc_layout(key)[1]


def draw_qkv_weight(key, part):
    base = jax.random.normal(jax.random.fold_in(key, 11), (D, 3, D), jnp.float32) * D ** (-0.5)
    return base


def block_levels(own_key, dims, cuts, least, high):
    level = 1.0
    for dim, parts in cuts:
        heights = jax.random.uniform(jax.random.fold_in(jax.random.fold_in(own_key, 6), dim), (parts,), jnp.float32, least / len(cuts), high / len(cuts))
        level = level * jnp.repeat(jnp.exp(heights), dims[dim] // parts).reshape((-1,) + (1,) * (len(dims) - 1 - dim))
    return level


def noise(stream_key, shape, spread, limit, cuts=(), held_as=jnp.bfloat16):
    entries = spread * jax.random.normal(stream_key, shape, jnp.float32)
    if cuts:
        entries = entries * block_levels(stream_key, shape, cuts, -0.22, 0.18)
    return jnp.clip(entries, -limit, limit).astype(held_as)


def setup_inputs(seed: int = 0) -> dict:
    seeds = jax.random.split(jax.random.key(seed), 11)
    tokens = noise(seeds[0], (TOKENS, D), 1.0, 6.0, ((0, 16),), jnp.float32)
    cotangent = noise(seeds[1], (TOKENS, D), 1.0, 6.0, ((0, 16),), jnp.float32)
    ln1_gain = jnp.clip(1.0 + 0.1 * jax.random.normal(seeds[2], (D,), jnp.float32), 0.5, 1.5)
    qkv_weight = draw_qkv_weight(jax.random.fold_in(seeds[10], 71), 0)
    attn_out_weight = noise(seeds[4], (D, D), (max(D // 256, 1)) ** -0.5, 3.0, ((0, 2), (1, 16)), jnp.float32)
    ln2_gain = jnp.clip(1.0 + 0.1 * jax.random.normal(seeds[5], (D,), jnp.float32), 0.5, 1.5)
    ff_in_weight = noise(seeds[6], (D, 2, FF), D ** -0.5, 0.1875, ((0, 16), (2, 2)), jnp.float32)
    ff_out_weight = noise(seeds[7], (FF, D), FF ** -0.5, 0.125, ((0, 2), (1, 16)), jnp.float32)
    segment_ids = draw_segment_ids(jax.random.fold_in(seeds[10], 71), 0)
    positions = draw_positions(jax.random.fold_in(seeds[10], 71), 0)
    return dict(tokens=tokens, cotangent=cotangent, ln1_gain=ln1_gain, qkv_weight=qkv_weight, attn_out_weight=attn_out_weight, ln2_gain=ln2_gain, ff_in_weight=ff_in_weight, ff_out_weight=ff_out_weight, segment_ids=segment_ids, positions=positions)


epsilon = 1e-05
rope_base = 160000.0
masked_score = -1e+30

def exact_dot(left, right):
    return jnp.dot(left, right, precision=lax.Precision.HIGHEST, preferred_element_type=jnp.float32)

def layer_norm(values_in, gain):
    center = values_in - lax.optimization_barrier(jnp.mean(values_in, -1, keepdims=True))
    inverse = lax.rsqrt(lax.optimization_barrier(jnp.mean(center * center, -1, keepdims=True)) + epsilon)
    return center * inverse * gain

def rope_tables(position_ids):
    half_dim = HD // 2
    freqs = jnp.power(rope_base, -(jnp.arange(half_dim, dtype=jnp.float32) * 2.0 / HD))
    angles = position_ids.astype(jnp.float32)[:, None] * freqs[None, :]
    both = jnp.concatenate([angles, angles], -1)
    return (jnp.cos(both), jnp.sin(both))

def rotate(vectors, cosine, sine_part):
    half_dim = HD // 2
    turned = jnp.concatenate([-vectors[..., half_dim:], vectors[..., :half_dim]], -1)
    return vectors * cosine[:, None, :] + turned * sine_part[:, None, :]

def forward_seq(tokens, ln1_gain, qkv_weight, attn_out_weight, ln2_gain, ff_in_weight, ff_out_weight, seg_row, pos_row):
    normed1 = layer_norm(tokens, ln1_gain)
    joined = exact_dot(normed1, qkv_weight.reshape(D, 3 * D)).reshape(SEQ, 3, H, HD)
    cosine, sine_part = rope_tables(pos_row)
    queries = rotate(joined[:, 0], cosine, sine_part)
    keys_rot = rotate(joined[:, 1], cosine, sine_part)
    values = joined[:, 2]
    scores = jnp.einsum('qhd,khd->hqk', queries, keys_rot, precision=lax.Precision.HIGHEST) / jnp.sqrt(jnp.float32(HD))
    same_doc = seg_row[:, None] == seg_row[None, :]
    scores = jnp.where(same_doc[None], scores, masked_score)
    attn_probs = jax.nn.softmax(scores, -1)
    attended = jnp.einsum('hqk,khd->qhd', attn_probs, values, precision=lax.Precision.HIGHEST).reshape(SEQ, D)
    residual_stream = tokens + exact_dot(attended, attn_out_weight)
    normed2 = layer_norm(residual_stream, ln2_gain)
    projected = exact_dot(normed2, ff_in_weight.reshape(D, 2 * FF)).reshape(SEQ, 2, FF)
    mixed_units = jax.nn.gelu(projected[:, 0], approximate=False) * projected[:, 1]
    return residual_stream + exact_dot(mixed_units, ff_out_weight)

def reference(tokens, cotangent, ln1_gain, qkv_weight, attn_out_weight, ln2_gain, ff_in_weight, ff_out_weight, segment_ids, positions):
    weights_all = (ln1_gain, qkv_weight, attn_out_weight, ln2_gain, ff_in_weight, ff_out_weight)
    token_seqs = tokens.reshape(SEQS, SEQ, D)
    grad_seqs = cotangent.reshape(SEQS, SEQ, D)

    def step(carry, item):
        token_row, grad_row, seg_row, pos_row = item

        def layer(token_in, first_norm_gain, qkv_in, attn_in, second_norm_gain, ffin_in, ffout_in):
            return forward_seq(token_in, first_norm_gain, qkv_in, attn_in, second_norm_gain, ffin_in, ffout_in, seg_row, pos_row)
        result, pullback = jax.vjp(layer, token_row, *weights_all)
        grads = pullback(grad_row)
        summed = tuple((old + new for old, new in zip(carry, grads[1:])))
        return (summed, (result, grads[0]))
    start = tuple((jnp.zeros_like(weight) for weight in weights_all))
    sums, (results, input_rows) = lax.scan(step, start, (token_seqs, grad_seqs, segment_ids, positions))
    return (results.reshape(TOKENS, D), input_rows.reshape(TOKENS, D), sums[0], sums[1], sums[2], sums[3], sums[4], sums[5])
```

```python
import functools

import jax
import jax.numpy as jnp
from jax import lax
from jax.experimental import pallas as pl
from jax.experimental.pallas import tpu as pltpu
from jax.sharding import PartitionSpec as P

HD = 64


epsilon = 1e-05
rope_base = 160000.0
masked_score = -1e30

def split(x):
    hi = x.astype(jnp.bfloat16)
    lo = (x - hi.astype(jnp.float32)).astype(jnp.bfloat16)
    return hi, lo

def mm(left, right):
    return jnp.dot(left, right, preferred_element_type=jnp.float32)

def mm_t(left, right):
    return lax.dot_general(left, right, (((1,), (1,)), ((), ())), preferred_element_type=jnp.float32)

def swap(x):
    return pltpu.roll(x, HD, 1)

def lanes(shape):
    return lax.broadcasted_iota(jnp.int32, shape, 1)

def turn_lanes(x):
    half = HD // 2
    up = pltpu.roll(x, 2 * HD - half, 1)
    down = pltpu.roll(x, half, 1)
    first = (lanes(x.shape) % HD) < half
    return up, down, first

def rope_in(x, cosine, sine):
    up, down, first = turn_lanes(x)
    return x * cosine + jnp.where(first, -up, down) * sine

def rope_out(y, cosine, sine):
    up, down, first = turn_lanes(y * sine)
    return y * cosine + jnp.where(first, up, -down)

def hi_lo_f32(x):
    hi = x.astype(jnp.bfloat16).astype(jnp.float32)
    return hi, x - hi

def packed(x, head):
    hi, lo = hi_lo_f32(x)
    low = lanes(x.shape) < HD
    if head == 0:
        return jnp.where(low, hi, swap(lo))
    return jnp.where(low, swap(hi), lo)

def doubled(p):
    low = lanes(p.shape) < HD
    s = swap(p)
    return jnp.where(low, p, s), jnp.where(low, s, p)

def left_cat(p):
    b = p.astype(jnp.bfloat16)
    return jnp.concatenate([b, b], 1)

def right_cat(p):
    a, b = doubled(p)
    return jnp.concatenate([a.astype(jnp.bfloat16), b.astype(jnp.bfloat16)], 1)

def fold(x):
    return x + swap(x)

def attn_fwd_kernel(q_ref, k_ref, v_ref, cos_ref, sin_ref, segc_ref, segr_ref, out_ref, lse_ref):
    cosine, sine = cos_ref[...], sin_ref[...]
    q = rope_in(q_ref[...], cosine, sine) * 0.125
    k = rope_in(k_ref[...], cosine, sine)
    v = v_ref[...]
    keep = segc_ref[...] == segr_ref[0]
    outs, lses = [], []
    for head in range(2):
        s = mm_t(left_cat(packed(q, head)), right_cat(packed(k, head)))
        s = jnp.where(keep, s, masked_score)
        m = jnp.max(s, 1, keepdims=True)
        e = jnp.exp(s - m)
        total = jnp.sum(e, 1, keepdims=True)
        hi, lo = split(e)
        vb = packed(v, head).astype(jnp.bfloat16)
        outs.append(fold(mm(hi, vb) + mm(lo, vb)) / total)
        lses.append(m + jnp.log(total))
    low = lanes(v.shape) < HD
    out_ref[...] = jnp.where(low, outs[0], outs[1])
    lse_ref[...] = jnp.where(low, lses[0], lses[1])

def attn_bwd_kernel(q_ref, k_ref, v_ref, cos_ref, sin_ref, segc_ref, segr_ref, out_ref, lse_ref, do_ref, dj_ref):
    cosine, sine = cos_ref[...], sin_ref[...]
    q = rope_in(q_ref[...], cosine, sine) * 0.125
    k = rope_in(k_ref[...], cosine, sine)
    v = v_ref[...]
    d_out = do_ref[...]
    prod = d_out * out_ref[...]
    lse = lse_ref[...]
    keep = segc_ref[...] == segr_ref[0]
    low = lanes(v.shape) < HD
    dqs, dks, dvs = [], [], []
    for head in range(2):
        qp, kp, vp, dp_ = packed(q, head), packed(k, head), packed(v, head), packed(d_out, head)
        s = mm_t(left_cat(qp), right_cat(kp))
        s = jnp.where(keep, s, masked_score)
        mine = low if head == 0 else jnp.logical_not(low)
        delta = jnp.sum(jnp.where(mine, prod, 0.0), 1, keepdims=True)
        lse_h = lse[:, head * HD : head * HD + 1]
        p = jnp.exp(s - lse_h)
        d_p = mm_t(left_cat(dp_), right_cat(vp))
        ds = p * (d_p - delta)
        p_hi, p_lo = split(p)
        ds_hi, ds_lo = split(ds)
        kb = kp.astype(jnp.bfloat16)
        dqs.append(fold(mm(ds_hi, kb) + mm(ds_lo, kb)))
        qt = jnp.transpose(qp).astype(jnp.bfloat16)
        dt = jnp.transpose(dp_).astype(jnp.bfloat16)
        dk = mm(qt, ds_hi) + mm(qt, ds_lo)
        dv = mm(dt, p_hi) + mm(dt, p_lo)
        dks.append(dk[:HD] + dk[HD:])
        dvs.append(dv[:HD] + dv[HD:])
    dq = jnp.where(low, dqs[0], dqs[1]) * 0.125
    dk = jnp.transpose(jnp.concatenate(dks, 0))
    dv = jnp.transpose(jnp.concatenate(dvs, 0))
    dj_ref[0] = rope_out(dq, cosine, sine)
    dj_ref[1] = rope_out(dk, cosine, sine)
    dj_ref[2] = dv

def attn_specs(seq_len, pairs, first=0):
    col = lambda off: pl.BlockSpec((seq_len, 2 * HD), lambda s, h: (s, h + off + first))
    table = pl.BlockSpec((seq_len, 2 * HD), lambda s, h: (s, 0))
    segc = pl.BlockSpec((seq_len, 1), lambda s, h: (s, 0))
    segr = pl.BlockSpec((1, 1, seq_len), lambda s, h: (s, 0, 0))
    return col, [col(0), col(pairs), col(2 * pairs), table, table, segc, segr]

def attn_fwd(joined, cosine, sine, segc, segr):
    seqs, _, seq_len = segr.shape
    width = joined.shape[1] // 3
    pairs = width // (2 * HD)
    col, specs = attn_specs(seq_len, pairs)
    shape = jax.ShapeDtypeStruct((seqs * seq_len, width), jnp.float32)
    return pl.pallas_call(
        attn_fwd_kernel, grid=(seqs, pairs), in_specs=specs, out_specs=[col(0), col(0)],
        out_shape=[shape, shape], name="attn_fwd",
    )(joined, joined, joined, cosine, sine, segc, segr)

def attn_bwd(joined, cosine, sine, segc, segr, out, lse, d_out, first, taken):
    seqs, _, seq_len = segr.shape
    width = joined.shape[1] // 3
    pairs = width // (2 * HD)
    col, specs = attn_specs(seq_len, pairs, first)
    return pl.pallas_call(
        attn_bwd_kernel, grid=(seqs, taken), in_specs=specs + [col(0)] * 3,
        out_specs=pl.BlockSpec((3, seq_len, 2 * HD), lambda s, h: (0, s, h)),
        out_shape=jax.ShapeDtypeStruct((3, seqs * seq_len, taken * 2 * HD), jnp.float32),
        name="attn_bwd",
    )(joined, joined, joined, cosine, sine, segc, segr, out, lse, d_out)


def dims_dot(left, right, over):
    return lax.dot_general(
        left,
        right,
        (over, ((), ())),
        precision=lax.Precision.HIGH,
        preferred_element_type=jnp.float32,
    )


def plain_dot(left, right):
    return dims_dot(left, right, ((1,), (0,)))


def normalize_rows(values_in):
    center = values_in - jnp.mean(values_in, -1, keepdims=True)
    inverse = lax.rsqrt(jnp.mean(center * center, -1, keepdims=True) + epsilon)
    return (center * inverse, inverse)


def norm_back(grad_out, normed, inverse):
    first = jnp.mean(grad_out, -1, keepdims=True)
    second = jnp.mean(grad_out * normed, -1, keepdims=True)
    return inverse * (grad_out - first - normed * second)


def rope_tables(position_ids):
    half_dim = HD // 2
    freqs = jnp.power(rope_base, -(jnp.arange(half_dim, dtype=jnp.float32) * 2.0 / HD))
    angles = position_ids.astype(jnp.float32)[:, None] * freqs[None, :]
    return (jnp.tile(jnp.cos(angles), (1, 4)), jnp.tile(jnp.sin(angles), (1, 4)))


def ring_order(mesh):
    devices = mesh.devices
    count = devices.shape[0] // 2
    spots = [getattr(devices[2 * j, 0], "coords", None) for j in range(count)]
    if any(s is None for s in spots) or len(set(map(tuple, spots))) != count:
        return tuple(range(count))
    axes = [a for a in range(len(spots[0])) if len({s[a] for s in spots}) > 1]
    if len(axes) != 2:
        return tuple(range(count))
    axes.sort(key=lambda a: -len({s[a] for s in spots}))
    longs = sorted({s[axes[0]] for s in spots})
    shorts = sorted({s[axes[1]] for s in spots})
    where = {(s[axes[0]], s[axes[1]]): j for j, s in enumerate(spots)}
    if len(where) != count or len(longs) * len(shorts) != count or len(longs) % 2:
        return tuple(range(count))
    path = [(a, shorts[0]) for a in longs]
    for n, a in enumerate(reversed(longs)):
        path += [(a, b) for b in (shorts[1:] if n % 2 == 0 else shorts[:0:-1])]
    return tuple(where[p] for p in path)


class Ring:
    def __init__(self, order):
        self.order = order
        self.count = len(order)
        places = [0] * self.count
        for place, chip in enumerate(order):
            places[chip] = place
        index = lax.axis_index("dp")
        self.core = index % 2
        self.place = jnp.asarray(places, jnp.int32)[index // 2]
        self.chips = jnp.asarray(order, jnp.int32)

    def chip_at(self, step):
        return self.chips[(self.place + step) % self.count]

    def hop(self, values, step):
        pairs = []
        for place, chip in enumerate(self.order):
            target = self.order[(place + step) % self.count]
            pairs += [(2 * chip + core, 2 * target + core) for core in range(2)]
        return lax.ppermute(values, "dp", pairs)

    def sibling(self, values):
        return lax.ppermute(values, "dp", [(i, i ^ 1) for i in range(2 * self.count)])

    def blocks(self, core):
        return 2 * self.chips[(self.place + jnp.arange(self.count)) % self.count] + core

    def start(self, turned, *rights):
        return self.sibling(grad_rows(turned, rights, self.blocks(1 - self.core), None))

    def keep(self, turned, received, *rights):
        return Chain(self, grad_rows(turned, rights, self.blocks(self.core), received))


class Chain:
    def __init__(self, ring, parts):
        self.ring, self.parts, self.step = ring, parts, 0
        self.half = parts.shape[1] // 2
        count = ring.count
        self.ahead, self.back = parts[count - 1, : self.half], parts[1, self.half :]

    def moved(self):
        ring, count = self.ring, self.ring.count
        self.step += 1
        self.ahead = ring.hop(self.ahead, 1)
        self.back = ring.hop(self.back, -1)
        ahead_at, back_at = (-self.step - 1) % count, (self.step + 1) % count
        self.ahead = self.ahead + self.parts[ahead_at, : self.half]
        self.back = self.back + self.parts[back_at, self.half :]
        return (self.ahead, self.back)

    def total(self):
        while self.step < self.ring.count - 1:
            self.moved()
        return jnp.concatenate([self.ahead, self.back], 0)


def grad_kernel(rights, table, left_ref, *rest):
    out_ref, rest = rest[-1], rest[:-1]
    rest, extra = rest[:rights], rest[rights:]
    right = jnp.concatenate([r[i] for i in range(rest[0].shape[0]) for r in rest], 1)
    count, shard, _ = out_ref.shape
    first = pl.program_id(0) * count
    rows = [
        left_ref[pl.ds(pl.multiple_of(table[first + p] * shard, shard), shard), :]
        for p in range(count)
    ]
    total = mm3(split(jnp.concatenate(rows, 0)), split(right), mm)
    total = total.reshape(out_ref.shape)
    if extra:
        total = total + extra[0][...]
    out_ref[...] = total


def grad_rows(turned, rights, table, extra):
    width, tokens = turned.shape
    count = table.shape[0]
    shard = width // (2 * count)
    columns = sum(r.shape[0] * r.shape[2] for r in rights)
    steps = 2
    tile = pl.BlockSpec((count // steps, shard, columns), lambda i, table: (i, 0, 0))
    specs = [
        pl.BlockSpec((width, tokens), lambda i, table: (0, 0)),
    ] + [pl.BlockSpec(r.shape, lambda i, table: (0, 0, 0)) for r in rights]
    args = [turned] + list(rights)
    if extra is not None:
        specs.append(tile)
        args.append(extra)
    return pl.pallas_call(
        functools.partial(grad_kernel, len(rights)),
        grid_spec=pltpu.PrefetchScalarGridSpec(
            num_scalar_prefetch=1, grid=(steps,), in_specs=specs, out_specs=tile
        ),
        out_shape=jax.ShapeDtypeStruct((count, shard, columns), jnp.float32),
        name="grad_rows",
    )(table, *args)


def after(values, *others):
    return lax.optimization_barrier((values,) + others)[0]

def mm3(a, b, product):
    a_hi, a_lo = a
    b_hi, b_lo = b
    return product(a_hi, b_hi) + (product(a_hi, b_lo) + product(a_lo, b_hi))


def rows_of(ref):
    return ref[...].reshape(-1, ref.shape[-1])


def residual_kernel(x_ref, a_ref, w_ref, res_ref, xhat_ref, inv_ref):
    res = x_ref[...] + mm3(split(a_ref[...]), split(w_ref[...]), mm_t)
    center = res - jnp.mean(res, 1, keepdims=True)
    inverse = lax.rsqrt(jnp.mean(center * center, 1, keepdims=True) + epsilon)
    res_ref[...] = res
    xhat_ref[...] = center * inverse
    inv_ref[...] = inverse


def residual_norm(tokens, attended, early):
    rows, width = tokens.shape
    tile = pl.BlockSpec((rows // 2, width), lambda i: (i, 0))
    full = jax.ShapeDtypeStruct((rows, width), jnp.float32)
    return pl.pallas_call(
        residual_kernel,
        grid=(2,),
        in_specs=[tile, tile, pl.BlockSpec((width, width), lambda i: (0, 0))],
        out_specs=[tile, tile, pl.BlockSpec((rows // 2, 1), lambda i: (i, 0))],
        out_shape=[full, full, jax.ShapeDtypeStruct((rows, 1), jnp.float32)],
        name="residual_norm",
    )(tokens, attended, early)


def ffn_kernel(x_ref, c_ref, wi_ref, wg_ref, wo_ref, mixed_ref, di_ref, dg_ref, xh, xl, ch, cl):
    @pl.when(pl.program_id(0) == 0)
    def _():
        xh[...], xl[...] = split(x_ref[...])
        ch[...], cl[...] = split(c_ref[...])

    x, c = (xh[...], xl[...]), (ch[...], cl[...])
    inner = mm3(x, split(rows_of(wi_ref)), mm)
    gate = mm3(x, split(rows_of(wg_ref)), mm)
    d_mixed = mm3(c, split(rows_of(wo_ref)), mm)
    below = 0.5 * (1.0 + lax.erf(inner * 0.7071067811865476))
    slope = below + inner * (jnp.exp(-0.5 * inner * inner) * 0.3989422804014327)
    curved = inner * below
    mixed_ref[...] = curved * gate
    di_ref[...] = d_mixed * gate * slope
    dg_ref[...] = d_mixed * curved


def ffn(normed, cotangent, late):
    rows, width = normed.shape
    blocks, _, shard, hidden = late.shape
    tile = min(384, hidden)
    whole = pl.BlockSpec((rows, width), lambda j: (0, 0), pipeline_mode=pl.Buffered(1))
    weight = lambda i: pl.BlockSpec((blocks, None, shard, tile), lambda j: (0, i, 0, j))
    out = pl.BlockSpec((rows, tile), lambda j: (0, j))
    shape = jax.ShapeDtypeStruct((rows, hidden), jnp.float32)
    half = pltpu.VMEM((rows, width), jnp.bfloat16)
    return pl.pallas_call(
        ffn_kernel,
        grid=(pl.cdiv(hidden, tile),),
        in_specs=[whole, whole, weight(0), weight(1), weight(2)],
        out_specs=[out] * 3,
        out_shape=[shape] * 3,
        scratch_shapes=[half] * 4,
        name="ffn",
    )(normed, cotangent, late, late, late)


def back_kernel(*refs):
    count = (len(refs) - 1) // 4
    lefts, weights, out_ref, halves = (
        refs[:count],
        refs[count : 2 * count],
        refs[2 * count],
        refs[2 * count + 1 :],
    )

    @pl.when(pl.program_id(0) == 0)
    def _():
        for i, left in enumerate(lefts):
            halves[2 * i][...], halves[2 * i + 1][...] = split(left[...])

    total = None
    for i, weight in enumerate(weights):
        part = mm3((halves[2 * i][...], halves[2 * i + 1][...]), split(rows_of(weight)), mm_t)
        total = part if total is None else total + part
    out_ref[...] = total


def back_rows(lefts, weights, specs, left_specs, columns, tile):
    rows = lefts[0].shape[-2]
    halves = []
    for spec in left_specs:
        shape = tuple(d for d in spec.block_shape if d is not None)
        halves += [pltpu.VMEM(shape, jnp.bfloat16)] * 2
    return pl.pallas_call(
        back_kernel,
        grid=(columns // tile,),
        in_specs=list(left_specs) + list(specs),
        out_specs=pl.BlockSpec((rows, tile), lambda j: (0, j)),
        out_shape=jax.ShapeDtypeStruct((rows, columns), jnp.float32),
        scratch_shapes=halves,
        name="back_rows",
    )(*lefts, *weights)


def ff_back(lefts, late, which, part, parts):
    blocks, _, shard, hidden = late.shape
    columns = blocks * shard // parts
    tile = max(256, shard)
    step = tile // shard
    offset = part * columns // tile
    left = pl.BlockSpec(lefts[0].shape, lambda j: (0, 0), pipeline_mode=pl.Buffered(1))
    specs = [
        pl.BlockSpec((step, None, shard, hidden), lambda j, i=i: (j + offset, i, 0, 0))
        for i in which
    ]
    return back_rows(lefts, [late] * len(lefts), specs, [left] * len(lefts), columns, tile)


def qkv_back(d_cuts, early, offset):
    width = early.shape[0]
    _, rows, cut_width = d_cuts[0].shape
    cuts = len(d_cuts)
    lefts, left_specs, specs = [], [], []
    for i in range(3):
        for c, d in enumerate(d_cuts):
            lefts.append(d)
            left_specs.append(
                pl.BlockSpec((None, rows, cut_width), lambda j, i=i: (i, 0, 0), pipeline_mode=pl.Buffered(1))
            )
            at = offset // cut_width + i * cuts + c
            specs.append(pl.BlockSpec((256, cut_width), lambda j, at=at: (j, at)))
    return back_rows(lefts, [early] * len(lefts), specs, left_specs, width, 256)


def on_device(
    order,
    tokens,
    cotangent,
    ln1_gain,
    qkv_weight,
    attn_out_weight,
    ln2_gain,
    ff_in_weight,
    ff_out_weight,
    segment_ids,
    positions,
):
    ring = Ring(order)
    groups = lax.axis_size("tensor")
    group_here = lax.axis_index("tensor")
    shard, _, local_width = qkv_weight.shape
    ff_here = ff_in_weight.shape[2]
    row_count, model_width = tokens.shape

    def swap_groups(values):
        return lax.ppermute(values, "tensor", [(0, 1), (1, 0)])

    def group_sum(values):
        if groups == 2:
            return values + swap_groups(values)
        return lax.psum(values, "tensor")

    def swap_or_none(values):
        return swap_groups(values) if groups == 2 else None

    def joined_sum(values, other):
        return lax.psum(values, "tensor") if other is None else values + other

    def group_columns(values):
        if groups == 2:
            other = swap_groups(values)
            first = group_here == 0
            return jnp.concatenate(
                [jnp.where(first, values, other), jnp.where(first, other, values)], 1
            )
        return lax.all_gather(values, "tensor", axis=1, tiled=True)

    qkv_flat = qkv_weight.reshape(shard, 3 * local_width)
    attn_shard = group_columns(attn_out_weight.T)
    early_shard = jnp.concatenate([attn_shard, ln1_gain[:, None] * qkv_flat], 1)
    in_flat = ff_in_weight.transpose(1, 0, 2)
    late_shard = jnp.concatenate(
        [ln2_gain[None, :, None] * in_flat, ff_out_weight.T[None]], 0
    )
    early = lax.all_gather(early_shard, "dp", axis=0, tiled=True)
    late = lax.all_gather(late_shard, "dp", axis=0)
    w_qkv = early[:, model_width:]

    cosine, sine = rope_tables(positions.reshape(-1))
    segc, segr = segment_ids.reshape(-1, 1), segment_ids[:, None, :]
    first_normed, first_inverse = normalize_rows(tokens)
    first_turned, cot_turned = first_normed.T, cotangent.T
    joined = plain_dot(first_normed, w_qkv)
    attended, log_total = attn_fwd(joined, cosine, sine, segc, segr)
    residual, second_normed, second_inverse = residual_norm(
        tokens, group_columns(attended), early
    )
    second_turned = second_normed.T
    mixed, d_inner, d_gate = ffn(second_normed, cotangent, late)
    got_out = ring.start(cot_turned, mixed[None])
    d_parts, others = [], []
    wait = got_out
    for part in range(2):
        lefts = after((d_inner, d_gate), wait)
        d_parts.append(ff_back(lefts, late, (0, 1), part, 2))
        others.append(swap_groups(d_parts[-1]) if groups == 2 else None)
        if part == 0:
            chain_out = ring.keep(cot_turned, got_out, after(mixed, d_parts)[None])
            wait = chain_out.parts
    wait = (d_parts, chain_out.moved())
    got_inner = ring.start(second_turned, after(d_inner, wait)[None])
    got_gate = ring.start(second_turned, after(d_gate, got_inner, chain_out.moved())[None])
    chain_inner = ring.keep(second_turned, got_inner, after(d_inner, got_gate)[None])
    chain_gate = ring.keep(
        second_turned, got_gate, after(d_gate, chain_inner.parts, chain_out.moved())[None]
    )
    chains = [chain_out, chain_inner, chain_gate]

    def moved():
        return [c.moved() for c in chains if c.step < ring.count - 1]

    wait = (chain_gate.parts, moved())
    out_part = ff_back([after(mixed, wait)], late, (2,), 0, 1)
    wait = (out_part, moved())
    wait = (wait, moved())
    d_parts, others, out_part = after((d_parts, others, out_part), wait)
    d_second = jnp.concatenate([joined_sum(d, o) for d, o in zip(d_parts, others)], 1)
    d_resid = cotangent + norm_back(d_second, second_normed, second_inverse)
    result = residual + group_sum(after(out_part, d_second))
    w_attn_here = lax.dynamic_slice_in_dim(early, group_here * local_width, local_width, 1)
    d_attended = plain_dot(d_resid, w_attn_here)
    wait = (d_attended, moved())
    resid_turned = d_resid.T
    got_attn = ring.start(resid_turned, after(attended, wait)[None])
    chain_attn = ring.keep(resid_turned, got_attn, after(attended, got_attn)[None])
    wait = (chain_attn.parts, moved())
    chains.append(chain_attn)
    pairs = local_width // (2 * HD)
    cuts = 2 if pairs % 2 == 0 else 1
    d_cuts = []
    for cut in range(cuts):
        d_cuts.append(
            attn_bwd(
                joined, cosine, sine, segc, segr, attended, log_total,
                after(d_attended, wait), cut * pairs // cuts, pairs // cuts,
            )
        )
        wait = (d_cuts[-1], moved())
    d_first_part = qkv_back(after(d_cuts, wait), early, model_width)
    wait = (d_first_part, moved())
    got_qkv = ring.start(first_turned, *after(d_cuts, wait))
    chain_qkv = ring.keep(first_turned, got_qkv, *after(d_cuts, moved()))
    d_first = group_sum(d_first_part)
    out_grad, inner_grad, gate_grad, attn_grad = (c.total() for c in chains)
    qkv_grad = chain_qkv.total()
    d_tokens = d_resid + norm_back(d_first, first_normed, first_inverse)
    gain_two_out = group_sum(jnp.sum(in_flat[0] * inner_grad + in_flat[1] * gate_grad, 1))
    gain_one_out = group_sum(jnp.sum(qkv_flat * qkv_grad, 1))
    qkv_out = (ln1_gain[:, None] * qkv_grad).reshape(shard, 3, local_width)
    in_out = jnp.stack([ln2_gain[:, None] * inner_grad, ln2_gain[:, None] * gate_grad], 1)
    return (
        result,
        d_tokens,
        gain_one_out,
        qkv_out,
        attn_grad.T,
        gain_two_out,
        in_out,
        out_grad.T,
    )


def solution(mesh):
    order = ring_order(mesh)

    def run(*args):
        return on_device(order, *args)

    return jax.shard_map(
        run,
        mesh=mesh,
        in_specs=(
            P("dp", None),
            P("dp", None),
            P("dp"),
            P("dp", None, "tensor"),
            P("tensor", "dp"),
            P("dp"),
            P("dp", None, "tensor"),
            P("tensor", "dp"),
            P("dp", None),
            P("dp", None),
        ),
        out_specs=(
            P("dp", None),
            P("dp", None),
            P("dp"),
            P("dp", None, "tensor"),
            P("tensor", "dp"),
            P("dp"),
            P("dp", None, "tensor"),
            P("tensor", "dp"),
        ),
        check_vma=False,
    )
```
